512 devices in a mesh: grp: 2 (over core), blk: 128 (over z_lo, y, x), real: 2 (over z_hi).
Axes of the slice: x: 4, y: 8, z: 8 (z_hi: 2, z_lo: 4; z = z_hi * 4 + z_lo), core: 2. Of those that a mesh axis runs over, the one named last changes fastest.
Arguments:
- sky_data: float32 [32, 256, 8192], P('real', 'blk', 'grp'), may hold values from -6 to 6
- signal_prev: float32 [32, 256, 8192], P('real', 'blk', 'grp'), may hold values from -6 to 6
- noise_var: float32 [256, 8192], P('blk', 'grp'), may hold values from 1 to 16
- mask_flags: int32 [256, 8192], P('blk', 'grp'), may hold values 0 or 1
- cycle_table: int32 [256], P('blk'), may hold values from 0 to 255, each once
- m_table: int32 [512], replicated, may hold values from 0 to 4095, as said below
- spectrum: float32 [4096], P(('grp', 'real')), may hold values from 0.05 to 5
- legendre: bfloat16 [512, 4096, 256], P('blk', ('grp', 'real')), may hold values from -0.375 to 0.375
Outputs:
- wiener_alm: float32 [32, 2, 512, 4096], P(None, None, 'blk', ('grp', 'real'))
- signal_next: float32 [32, 256, 8192], P('real', 'blk', 'grp')
The draws below stay inside these ranges and needn't reach their ends.
Inputs may be any that keep to these rules, and one draw needn't show every extreme that they name: `m_table`: distinct orders; 0 and 4095 are always among them. `cycle_table`: each cycle number once.
All inputs are finite; a program needn't handle non-finite values. No bound on the sum of `mask_flags` on one device may be relied on, other than what follows from the above.
Results may differ from the reference program's by a relative error of at most 0.0063.
Values may be sent and summed in bfloat16 or wider, within the bound.
A program may use at most 64 MiB of HBM per device.

```python
import math
import jax
import jax.numpy as jnp
from jax import lax

NPHI = 8192
LBAND = 4096
NREAL = 32
CYCLES = 256
MWIN = 512


def draw_m_table(key, part):
    first_key = jax.random.fold_in(key, 11)
    second_key = jax.random.fold_in(key, 12)
    middle_ids = jax.random.permutation(first_key, LBAND - 2)[:MWIN - 2].astype(jnp.int32) + 1
    values = jnp.concatenate([jnp.array([0, LBAND - 1], dtype=jnp.int32), middle_ids])
    shuffle = jax.random.permutation(second_key, MWIN)
    return values[shuffle].astype(jnp.int32)


def place_ends(values, stream_key, smallest, largest):
    index_at = [jax.random.randint(jax.random.fold_in(stream_key, axis), (), 0, length) for axis, length in enumerate(values.shape)]
    widest = values.shape.index(max(values.shape))
    next_to = index_at[:widest] + [(index_at[widest] + 1) % values.shape[widest]] + index_at[widest + 1:]
    return values.at[tuple(index_at)].set(smallest).at[tuple(next_to)].set(largest)


def block_scale(own_key, extent, cuts, smallest, high):
    def one(dim, blocks):
        draws = jax.random.uniform(jax.random.fold_in(jax.random.fold_in(own_key, 6), dim), (blocks,), jnp.float32, smallest / len(cuts), high / len(cuts))
        return jnp.repeat(jnp.exp(draws), extent[dim] // blocks).reshape((-1,) + (1,) * (len(extent) - dim - 1))

    gain = one(*cuts[0])
    for cut in cuts[1:]:
        gain = gain * one(*cut)
    return gain


def gaussian(stream_key, extent, width, reach, shards=(), kind=jnp.bfloat16):
    result = jax.random.normal(stream_key, extent, jnp.float32) * width
    if len(shards) > 0:
        result = block_scale(stream_key, extent, shards, -0.22, 0.18) * result
    return jnp.clip(result, min=-reach, max=reach).astype(kind)


def setup_inputs(seed: int = 0) -> dict:
    arg_keys = jax.random.split(jax.random.key(seed), 9)
    sky_data = gaussian(arg_keys[0], (NREAL, CYCLES, NPHI), 1.0, 6.0, ((0, 2), (1, 128), (2, 2)), jnp.float32)
    signal_prev = gaussian(arg_keys[1], (NREAL, CYCLES, NPHI), 1.0, 6.0, ((0, 2), (1, 128), (2, 2)), jnp.float32)
    noise_var = jnp.clip(jnp.exp(math.log(16.0) - 2.7725887 * jax.random.uniform(arg_keys[2], (CYCLES, NPHI), jnp.float32) ** block_scale(arg_keys[2], (CYCLES, NPHI), ((0, 128), (1, 2)), -0.2, 0.2)), 1.0, 16.0)
    mask_flags = place_ends((jax.random.randint(arg_keys[3], (CYCLES, NPHI), 0, 5) < 4).astype(jnp.int32), jax.random.fold_in(arg_keys[3], 1), 0, 1)
    cycle_table = jax.random.permutation(arg_keys[4], CYCLES).astype(jnp.int32)
    m_table = draw_m_table(jax.random.fold_in(arg_keys[8], 71), 0)
    spectrum = jnp.clip(jnp.exp(math.log(5.0) - 4.6051702 * jax.random.uniform(arg_keys[6], (LBAND,), jnp.float32) ** block_scale(arg_keys[6], (LBAND,), ((0, 4),), -0.2, 0.2)), 0.05, 5.0)
    legendre = gaussian(arg_keys[7], (MWIN, LBAND, CYCLES), CYCLES ** -0.5, 0.375, ((0, 128), (1, 4)))
    return dict(sky_data=sky_data, signal_prev=signal_prev, noise_var=noise_var, mask_flags=mask_flags, cycle_table=cycle_table, m_table=m_table, spectrum=spectrum, legendre=legendre)


def phase_tables(col_ids, mode_ids, cycle_len):
    product_ids = (col_ids[:, None] * mode_ids[None, :]) % cycle_len
    angles = product_ids.astype(jnp.float32) * (2.0 * math.pi / cycle_len)
    return jnp.cos(angles).astype(jnp.bfloat16), jnp.sin(angles).astype(jnp.bfloat16)


def cycle_offsets(cycle_ids, mode_ids, cycle_len):
    parity = (cycle_ids % 2).astype(jnp.float32)
    shifts = (math.pi / cycle_len) * parity[:, None] * mode_ids[None, :].astype(jnp.float32)
    return jnp.cos(shifts), jnp.sin(shifts)


def reference(sky_data, signal_prev, noise_var, mask_flags, cycle_table, m_table, spectrum, legendre):
    weight = mask_flags.astype(jnp.float32) / (noise_var - 0.5)
    messenger = (weight * sky_data + 2.0 * signal_prev) / (weight + 2.0)
    cos_tab, sin_tab = phase_tables(jnp.arange(NPHI, dtype=jnp.int32), m_table, NPHI)
    cos_shift, sin_shift = cycle_offsets(cycle_table, m_table, NPHI)
    flat_rows = messenger.astype(jnp.bfloat16).reshape(NREAL * CYCLES, NPHI)
    base_cos = jnp.dot(flat_rows, cos_tab, preferred_element_type=jnp.float32).reshape(NREAL, CYCLES, MWIN)
    base_sin = -jnp.dot(flat_rows, sin_tab, preferred_element_type=jnp.float32).reshape(NREAL, CYCLES, MWIN)
    norm_scale = NPHI ** -0.5
    fourier_re = ((base_cos * cos_shift + base_sin * sin_shift) * norm_scale).astype(jnp.bfloat16)
    fourier_im = ((base_sin * cos_shift - base_cos * sin_shift) * norm_scale).astype(jnp.bfloat16)
    fourier = jnp.stack([fourier_re, fourier_im], 1)
    fourier_cols = fourier.transpose(3, 2, 0, 1).reshape(MWIN, CYCLES, NREAL * 2)
    factor = spectrum / (spectrum + 0.5)
    syn_scale = (CYCLES / LBAND) ** 0.5

    def per_order(operands):
        leg_order, fourier_col = operands
        coefficients = jnp.dot(leg_order, fourier_col, preferred_element_type=jnp.float32)
        filtered = coefficients * factor[:, None]
        synthesized = jnp.dot(leg_order.T, filtered.astype(jnp.bfloat16), preferred_element_type=jnp.float32) * syn_scale
        return filtered, synthesized

    filtered, synthesized = lax.map(per_order, (legendre, fourier_cols))
    wiener_alm = filtered.reshape(MWIN, LBAND, NREAL, 2).transpose(2, 3, 0, 1)
    rounded = lax.optimization_barrier(synthesized.astype(jnp.bfloat16))
    cycle_modes = rounded.astype(jnp.float32).reshape(MWIN, CYCLES, NREAL, 2)
    modes_re = cycle_modes[..., 0].transpose(2, 1, 0)
    modes_im = cycle_modes[..., 1].transpose(2, 1, 0)
    rotated_re = (modes_re * cos_shift - modes_im * sin_shift).astype(jnp.bfloat16)
    rotated_im = (modes_im * cos_shift + modes_re * sin_shift).astype(jnp.bfloat16)
    contract = (((1,), (1,)), ((), ()))
    pixel_sum = lax.dot_general(rotated_re.reshape(-1, MWIN), cos_tab, contract, preferred_element_type=jnp.float32)
    pixel_sum = pixel_sum - lax.dot_general(rotated_im.reshape(-1, MWIN), sin_tab, contract, preferred_element_type=jnp.float32)
    signal_next = (pixel_sum * MWIN ** -0.5).reshape(NREAL, CYCLES, NPHI)
    return wiener_alm, signal_next
```

```python
import math

import jax
import jax.numpy as jnp
from jax import lax
from jax.sharding import PartitionSpec as P


def copy_for_each(x, axis):
    peers = lax.axis_size(axis)
    return lax.all_to_all(jnp.broadcast_to(x[None], (peers, *x.shape)), axis, 0, 0, tiled=True)


def of_everyone(x, axis):
    everything = copy_for_each(x, axis)
    return jnp.sum(everything, axis=0)


def in_one(arrays, axis):
    ends = [0]
    for a in arrays:
        ends.append(ends[-1] + a.size)
    subtotal = of_everyone(jnp.concatenate([a.ravel() for a in arrays]), axis)
    return tuple((subtotal[b:e].reshape(a.shape) for a, b, e in zip(arrays, ends, ends[1:])))


def side_by_side(arrays, axis, split_dim, concat_dim, along):
    both = jnp.concatenate(arrays, axis=along)
    whole, at, finished = (
        lax.all_to_all(both, axis, split_axis=split_dim, concat_axis=concat_dim, tiled=True),
        0,
        [],
    )
    for a in arrays:
        finished.append(lax.slice_in_dim(whole, at, at + a.shape[along], axis=along))
        at += a.shape[along]
    return tuple(finished)


def in_one_piece(arrays, axis, dim, along):
    both = jnp.concatenate(arrays, axis=along)
    whole, at, finished = (lax.all_gather(both, axis, axis=dim, tiled=True), 0, [])
    for a in arrays:
        finished.append(lax.slice_in_dim(whole, at, at + a.shape[along], axis=along))
        at += a.shape[along]
    return tuple(finished)


def split_up(x, dim, peers):
    before, after = (x.shape[:dim], x.shape[dim + 1 :])
    return jnp.moveaxis(x.reshape(*before, peers, -1, *after), dim, 0)


def sum_at_owner(x, axis, dim):
    parts = split_up(x, dim, lax.axis_size(axis))
    arrived = lax.all_to_all(parts, axis, split_axis=0, concat_axis=0, tiled=True)
    return arrived.sum(axis=0)


def unit_circle(col_ids, mode_ids, cycle_len):
    product_ids = col_ids[:, None] * mode_ids[None, :] % cycle_len
    angles = product_ids.astype(jnp.float32) * (2.0 * math.pi / cycle_len)
    return jnp.cos(angles), jnp.sin(angles)


def phase_tables(first_col, half_len, mode_ids, cycle_len):
    fine_count = 64
    coarse_count = half_len // fine_count
    coarse_cols = first_col + fine_count * jnp.arange(coarse_count, dtype=jnp.int32)
    coarse_cos, coarse_sin = unit_circle(coarse_cols, mode_ids, cycle_len)
    fine_cos, fine_sin = unit_circle(
        jnp.arange(fine_count, dtype=jnp.int32), mode_ids, cycle_len
    )
    coarse_cos, coarse_sin, fine_cos, fine_sin = lax.optimization_barrier(
        (coarse_cos, coarse_sin, fine_cos, fine_sin)
    )
    a, b = coarse_cos[:, None], coarse_sin[:, None]
    c, d = fine_cos[None], fine_sin[None]
    cos_tab = (a * c - b * d).astype(jnp.bfloat16).reshape(half_len, -1)
    sin_tab = (b * c + a * d).astype(jnp.bfloat16).reshape(half_len, -1)
    return lax.optimization_barrier((cos_tab, sin_tab))


def cycle_offsets(cycle_ids, mode_ids, cycle_len):
    parity = (cycle_ids % 2).astype(jnp.float32)
    shifts = math.pi / cycle_len * parity[:, None] * mode_ids[None, :].astype(jnp.float32)
    return (jnp.cos(shifts), jnp.sin(shifts))


def forward_modes(re_part, im_part):
    summed = in_one((re_part, im_part), "grp")
    fourier_pair = (summed[0].astype(jnp.bfloat16), summed[1].astype(jnp.bfloat16))
    fourier_pair = side_by_side((fourier_pair[0], fourier_pair[1]), "blk", 2, 1, 0)
    fourier_pair = in_one_piece((fourier_pair[0], fourier_pair[1]), "real", 0, 1)
    return fourier_pair


def backward_cycles(partial_value):
    summed = sum_at_owner(partial_value, "real", 0)
    reduced = of_everyone(summed, "grp")
    cycle_pair = lax.all_to_all(
        reduced.astype(jnp.bfloat16), "blk", split_axis=2, concat_axis=3, tiled=True
    )
    return cycle_pair


def per_device(
    sky_data, signal_prev, noise_var, mask_flags, cycle_table, m_table, spectrum, legendre
):
    real_dev, cycle_dev, half_len = sky_data.shape
    cycle_len = half_len * lax.axis_size("grp")
    mode_count = m_table.shape[0]
    first_col = lax.axis_index("grp") * half_len
    cos_tab, sin_tab = phase_tables(first_col, half_len, m_table, cycle_len)
    cos_shift, sin_shift = cycle_offsets(cycle_table, m_table, cycle_len)
    weight = mask_flags.astype(jnp.float32) / (noise_var - 0.5)
    messenger = (weight * sky_data + 2.0 * signal_prev) / (weight + 2.0)
    flat_rows = messenger.astype(jnp.bfloat16).reshape(real_dev * cycle_dev, half_len)
    base_cos = jnp.dot(flat_rows, cos_tab, preferred_element_type=jnp.float32).reshape(
        real_dev, cycle_dev, mode_count
    )
    base_sin = -jnp.dot(flat_rows, sin_tab, preferred_element_type=jnp.float32).reshape(
        real_dev, cycle_dev, mode_count
    )
    norm_scale = cycle_len ** (-0.5)
    re_part = (base_cos * cos_shift + base_sin * sin_shift) * norm_scale
    im_part = (base_sin * cos_shift - base_cos * sin_shift) * norm_scale
    fourier_re, fourier_im = forward_modes(re_part, im_part)
    fourier = jnp.stack([fourier_re, fourier_im], 1)
    coefficients = jnp.einsum(
        "mlr,kcrm->kcml", legendre, fourier, preferred_element_type=jnp.float32
    )
    factor = spectrum / (spectrum + 0.5)
    wiener_alm = coefficients * factor
    total_l = legendre.shape[1] * lax.axis_size("grp") * lax.axis_size("real")
    syn_scale = (legendre.shape[2] / total_l) ** 0.5
    partial_value = (
        jnp.einsum(
            "mlr,kcml->kcrm",
            legendre,
            wiener_alm.astype(jnp.bfloat16),
            preferred_element_type=jnp.float32,
        )
        * syn_scale
    )
    cycle_pair = backward_cycles(partial_value)
    cycle_modes = cycle_pair.astype(jnp.float32)
    modes_re = cycle_modes[:, 0]
    modes_im = cycle_modes[:, 1]
    rotated_re = (modes_re * cos_shift - modes_im * sin_shift).astype(jnp.bfloat16)
    rotated_im = (modes_im * cos_shift + modes_re * sin_shift).astype(jnp.bfloat16)
    contract = (((1,), (1,)), ((), ()))
    pixel_sum = lax.dot_general(
        rotated_re.reshape(-1, mode_count), cos_tab, contract, preferred_element_type=jnp.float32
    )
    pixel_sum = pixel_sum - lax.dot_general(
        rotated_im.reshape(-1, mode_count), sin_tab, contract, preferred_element_type=jnp.float32
    )
    signal_next = (pixel_sum * mode_count ** (-0.5)).reshape(real_dev, cycle_dev, half_len)
    return (wiener_alm, signal_next)


def solution(mesh):
    in_specs = (
        P("real", "blk", "grp"),
        P("real", "blk", "grp"),
        P("blk", "grp"),
        P("blk", "grp"),
        P("blk"),
        P(),
        P(("grp", "real")),
        P("blk", ("grp", "real"), None),
    )
    out_specs = (P(None, None, "blk", ("grp", "real")), P("real", "blk", "grp"))
    return jax.shard_map(
        per_device, mesh=mesh, in_specs=in_specs, out_specs=out_specs, check_vma=False
    )
```

```python
import math

import jax
import jax.numpy as jnp
from jax import lax
from jax.experimental import pallas as pl
from jax.experimental.pallas import tpu as pltpu
from jax.sharding import PartitionSpec as P


def unit_circle(col_ids, mode_ids, cycle_len):
    product_ids = col_ids[:, None] * mode_ids[None, :] % cycle_len
    angles = product_ids.astype(jnp.float32) * (2.0 * math.pi / cycle_len)
    return jnp.cos(angles), jnp.sin(angles)


def phase_tables(first_col, half_len, mode_ids, cycle_len):
    fine_count = 64
    coarse_count = half_len // fine_count
    coarse_cols = first_col + fine_count * jnp.arange(coarse_count, dtype=jnp.int32)
    coarse_cos, coarse_sin = unit_circle(coarse_cols, mode_ids, cycle_len)
    fine_cos, fine_sin = unit_circle(
        jnp.arange(fine_count, dtype=jnp.int32), mode_ids, cycle_len
    )
    coarse_cos, coarse_sin, fine_cos, fine_sin = lax.optimization_barrier(
        (coarse_cos, coarse_sin, fine_cos, fine_sin)
    )
    a, b = coarse_cos[:, None], coarse_sin[:, None]
    c, d = fine_cos[None], fine_sin[None]
    cos_tab = (a * c - b * d).astype(jnp.bfloat16).reshape(half_len, -1)
    sin_tab = (b * c + a * d).astype(jnp.bfloat16).reshape(half_len, -1)
    return lax.optimization_barrier((cos_tab, sin_tab))


def cycle_offsets(cycle_ids, mode_ids, cycle_len):
    parity = (cycle_ids % 2).astype(jnp.float32)
    shifts = math.pi / cycle_len * parity[:, None] * mode_ids[None, :].astype(jnp.float32)
    return (jnp.cos(shifts), jnp.sin(shifts))


NX, NY, NZ = 4, 8, 8
NZL = 4
PLANE = NX * NY
MESH = pl.DeviceIdType.MESH
F32 = jnp.float32
BF16 = jnp.bfloat16


def dot_nn(a, b):
    return jnp.dot(a, b, preferred_element_type=F32)


def dot_nt(a, b):
    return lax.dot_general(a, b, (((1,), (1,)), ((), ())), preferred_element_type=F32)


def iotas(rows, cols):
    row = lax.broadcasted_iota(jnp.int32, (rows, cols), 0)
    col = lax.broadcasted_iota(jnp.int32, (rows, cols), 1)
    return row, col


def one_hot(match):
    return jnp.where(match, 1.0, 0.0).astype(BF16)


def order_rows(h):
    row, col = iotas(256, 128)
    return one_hot(((row >> 3) * 4 + (row & 3) == col) & (((row >> 2) & 1) == h))


def order_cols(h):
    row, col = iotas(128, 256)
    return one_hot(((col >> 3) * 4 + (col & 3) == row) & (((col >> 2) & 1) == h))


def order_first():
    row, col = iotas(256, 256)
    return one_hot(((col & 3) * 64 + ((col >> 2) & 1) * 32 + (col >> 3)) == row)


def order_last():
    row, col = iotas(256, 256)
    return one_hot(((row & 3) * 64 + ((row >> 2) & 1) * 32 + (row >> 3)) == col)


def cycle_order():
    row, col = iotas(256, 256)
    r, x, y, zl, h = row & 1, (row >> 1) & 3, (row >> 3) & 7, (row >> 6) & 1, row >> 7
    return one_hot(r * 128 + zl * 64 + h * 32 + x * 8 + y == col)


def exchange_kernel(
    syn_scale,
    part,
    leg,
    factor,
    wiener_out,
    modes_out,
    leg_p,
    gbuf,
    z_send,
    z_recv,
    y_send,
    y_recv,
    x_recv,
    bx_send,
    bx_recv,
    by_send,
    by_recv,
    bz_send,
    bz_recv,
    send_sem,
    recv_sem,
):
    g, b, zh = lax.axis_index("grp"), lax.axis_index("blk"), lax.axis_index("real")
    x, y, zl = b % NX, (b // NX) % NY, b // PLANE
    z = zh * NZL + zl
    other = 1 - g

    def device(core, zl_, y_, x_, zh_):
        return {"grp": core, "blk": zl_ * PLANE + y_ * NX + x_, "real": zh_}

    z_peers, y_peers, x_peers = [], [], []
    for d in range(1, NZ):
        z_ = (z + d) % NZ
        z_peers.append((z_ % NZL, z_ // NZL, device(g, z_ % NZL, y, x, z_ // NZL)))
    for d in range(1, NY):
        y_ = (y + d) % NY
        y_peers.append((y_, device(g, zl, y_, x, zh)))
    for d in range(NX):
        x_ = (x + d) % NX
        for core in (g, other):
            if d > 0 or core is other:
                x_peers.append((x_, core, device(core, zl, y, x_, zh)))
    core_peer = device(other, zl, y, x, zh)

    barrier = pltpu.get_barrier_semaphore()
    everyone = [p[-1] for p in z_peers] + [p[-1] for p in y_peers] + [p[-1] for p in x_peers]
    for peer in everyone:
        pl.semaphore_signal(barrier, inc=1, device_id=peer, device_id_type=MESH)

    permute = cycle_order()
    for s in range(4):
        leg_p[s] = dot_nn(leg[s], permute).astype(BF16)

    pl.semaphore_wait(barrier, len(everyone))

    sems = iter(range(64))

    def send(src, dst, peer):
        i = next(sems)
        copy = pltpu.make_async_remote_copy(
            src_ref=src,
            dst_ref=dst,
            send_sem=send_sem.at[i],
            recv_sem=recv_sem.at[i],
            device_id=peer,
            device_id_type=MESH,
        )
        copy.start()
        return copy

    sent = []

    def arrive(copies):
        for copy in copies:
            copy.wait_recv()
        sent.extend(copies)

    arrive([send(part.at[other], gbuf, core_peer)])
    for c in range(2):
        total = (part[g, c] + gbuf[c]).astype(BF16)
        for t in range(NZL):
            z_send[t, 16 * c : 16 * (c + 1)] = total[:, 128 * t : 128 * (t + 1)]
    copies = [send(z_send.at[p[0]], z_recv.at[zl, zh], p[2]) for p in z_peers]
    z_recv[zl, zh] = z_send[zl]
    arrive(copies)
    gathered = z_recv[...].reshape(256, 128)
    turned = dot_nt(order_rows(0), gathered[:128]) + dot_nt(order_rows(1), gathered[128:])
    y_send[...] = turned.astype(BF16).reshape(NY, NX, 8, 128)
    copies = [send(y_send.at[p[0]], y_recv.at[y], p[1]) for p in y_peers]
    y_recv[y] = y_send[y]
    arrive(copies)
    copies = [send(y_recv.at[:, p[0]], x_recv.at[g, x], p[2]) for p in x_peers]
    x_recv[g, x] = y_recv[:, x]
    arrive(copies)

    first = order_first()
    columns = [
        dot_nn(first, x_recv[r].reshape(256, 128)).T for r in range(2)
    ]
    scale = factor[...]
    back = []
    for s in range(4):
        rows = jnp.concatenate(
            [
                columns[r][64 * t : 64 * (t + 1), 64 * s : 64 * (s + 1)]
                for r in range(2)
                for t in range(2)
            ],
            axis=1,
        ).astype(BF16)
        wiener = dot_nt(rows, leg_p[s]) * scale
        wiener_out[s] = wiener
        back.append(dot_nn(wiener.astype(BF16), leg_p[s]) * syn_scale)
    last = order_last()
    for r in range(2):
        halves = [
            jnp.concatenate(
                [back[s][:, 128 * r + 64 * t : 128 * r + 64 * (t + 1)] for s in range(4)], axis=1
            )
            for t in range(2)
        ]
        turned = jnp.concatenate(halves, axis=0).T.astype(BF16)
        bx_send[r] = dot_nn(last, turned).astype(BF16).reshape(NX, NY, 8, 128)

    copies = [send(bx_send.at[p[1], p[0]], bx_recv.at[g, x], p[2]) for p in x_peers]
    bx_recv[g, x] = bx_send[g, x]
    arrive(copies)
    by_send[...] = (bx_recv[0].astype(F32) + bx_recv[1].astype(F32)).astype(BF16)
    copies = [send(by_send.at[:, p[0]], by_recv.at[y], p[1]) for p in y_peers]
    by_recv[y] = by_send[:, y]
    arrive(copies)
    plane = by_recv[...].reshape(256, 128)
    for h in range(2):
        turned = dot_nn(order_cols(h), plane).T.astype(BF16)
        bz_send[2 * h : 2 * h + 2] = turned.reshape(2, 2, 32, 128)
    copies = [send(bz_send.at[p[0], p[1]], bz_recv.at[zl, zh], p[2]) for p in z_peers]
    bz_recv[zl, zh] = bz_send[zl, zh]
    arrive(copies)
    for t in range(NZL):
        modes_out[g, :, 128 * t : 128 * (t + 1)] = (
            bz_recv[t, 0].astype(F32) + bz_recv[t, 1].astype(F32)
        ).astype(BF16)
    arrive([send(modes_out.at[g], modes_out.at[g], core_peer)])
    for copy in sent:
        copy.wait_send()


def exchange(part, legendre, factor, syn_scale):
    def vmem(shape, dtype=BF16):
        return pltpu.VMEM(shape, dtype)

    block = pl.BlockSpec(memory_space=pltpu.VMEM)
    plane = (NX, NY, 8, 128)
    return pl.pallas_call(
        lambda *refs: exchange_kernel(syn_scale, *refs),
        out_shape=(
            jax.ShapeDtypeStruct((4, 64, 1024), F32),
            jax.ShapeDtypeStruct((2, 32, 512), BF16),
        ),
        in_specs=[block] * 3,
        out_specs=(block, block),
        scratch_shapes=[
            vmem((4, 1024, 256)),
            vmem((2, 16, 512), F32),
            vmem((NZL, 32, 128)),
            vmem((NZL, 2, 32, 128)),
            vmem((NY, NX, 8, 128)),
            vmem((NY, NX, 8, 128)),
            vmem((2, NX, NY, 8, 128)),
            vmem((2, NX, NY, 8, 128)),
            vmem((2, NX, NY, 8, 128)),
            vmem((NX, NY, 8, 128)),
            vmem((NY, NX, 8, 128)),
            vmem((NZL, 2, 32, 128)),
            vmem((NZL, 2, 32, 128)),
            pltpu.SemaphoreType.DMA((64,)),
            pltpu.SemaphoreType.DMA((64,)),
        ],
        compiler_params=pltpu.CompilerParams(
            collective_id=0, has_side_effects=True, vmem_limit_bytes=40 * 1024 * 1024
        ),
    )(part, legendre, factor)


def per_device(
    sky_data, signal_prev, noise_var, mask_flags, cycle_table, m_table, spectrum, legendre
):
    real_dev, cycle_dev, half_len = sky_data.shape
    cycle_len = half_len * lax.axis_size("grp")
    mode_count = m_table.shape[0]
    first_col = lax.axis_index("grp") * half_len
    cos_tab, sin_tab = phase_tables(first_col, half_len, m_table, cycle_len)
    cos_shift, sin_shift = cycle_offsets(cycle_table, m_table, cycle_len)
    cos_rows, sin_rows = cos_shift[:, None], sin_shift[:, None]
    weight = mask_flags.astype(F32) / (noise_var - 0.5)
    messenger = (weight * sky_data + 2.0 * signal_prev) / (weight + 2.0)
    flat_rows = messenger.astype(BF16).transpose(1, 0, 2).reshape(-1, half_len)
    base_cos = dot_nn(flat_rows, cos_tab).reshape(cycle_dev, real_dev, mode_count)
    base_sin = -dot_nn(flat_rows, sin_tab).reshape(cycle_dev, real_dev, mode_count)
    norm_scale = cycle_len ** (-0.5)
    re_part = (base_cos * cos_rows + base_sin * sin_rows) * norm_scale
    im_part = (base_sin * cos_rows - base_cos * sin_rows) * norm_scale
    part = jnp.stack([re_part, im_part], 1)
    factor = (spectrum / (spectrum + 0.5))[None]
    total_l = legendre.shape[1] * lax.axis_size("grp") * lax.axis_size("real")
    syn_scale = (legendre.shape[2] / total_l) ** 0.5
    wiener, modes = exchange(part, legendre, factor, syn_scale)
    wiener_alm = (
        wiener.reshape(4, 2, 2, 16, 1024).transpose(1, 3, 2, 0, 4).reshape(32, 2, 4, 1024)
    )
    modes = modes.astype(F32).reshape(cycle_dev, 2, real_dev, mode_count)
    modes_re, modes_im = modes[:, 0], modes[:, 1]
    rotated_re = (modes_re * cos_rows - modes_im * sin_rows).astype(BF16)
    rotated_im = (modes_im * cos_rows + modes_re * sin_rows).astype(BF16)
    pixel_sum = dot_nt(rotated_re.reshape(-1, mode_count), cos_tab)
    pixel_sum = pixel_sum - dot_nt(rotated_im.reshape(-1, mode_count), sin_tab)
    signal_next = (pixel_sum * mode_count ** (-0.5)).reshape(cycle_dev, real_dev, half_len)
    return (wiener_alm, signal_next.transpose(1, 0, 2))


def solution(mesh):
    in_specs = (
        P("real", "blk", "grp"),
        P("real", "blk", "grp"),
        P("blk", "grp"),
        P("blk", "grp"),
        P("blk"),
        P(),
        P(("grp", "real")),
        P("blk", ("grp", "real"), None),
    )
    out_specs = (P(None, None, "blk", ("grp", "real")), P("real", "blk", "grp"))
    return jax.shard_map(
        per_device, mesh=mesh, in_specs=in_specs, out_specs=out_specs, check_vma=False
    )
```

```python
import math

import jax
import jax.numpy as jnp
from jax import lax
from jax.experimental import pallas as pl
from jax.experimental.pallas import tpu as pltpu
from jax.sharding import PartitionSpec as P


NX, NY, NZ = 4, 8, 8
NZL = 4
PLANE = NX * NY
BLOCKS = 8
SPAN = 512
ORDERS = 512
TURN = 16384
MESH = pl.DeviceIdType.MESH
F32 = jnp.float32
BF16 = jnp.bfloat16


def dot_nn(a, b):
    return jnp.dot(a, b, preferred_element_type=F32)


def dot_nt(a, b):
    return lax.dot_general(a, b, (((1,), (1,)), ((), ())), preferred_element_type=F32)


def iotas(rows, cols):
    row = lax.broadcasted_iota(jnp.int32, (rows, cols), 0)
    col = lax.broadcasted_iota(jnp.int32, (rows, cols), 1)
    return row, col


def one_hot(match):
    return jnp.where(match, 1.0, 0.0).astype(BF16)


def order_rows(h):
    row, col = iotas(256, 128)
    return one_hot(((row >> 3) * 4 + (row & 3) == col) & (((row >> 2) & 1) == h))


def order_cols(h):
    row, col = iotas(128, 256)
    return one_hot(((col >> 3) * 4 + (col & 3) == row) & (((col >> 2) & 1) == h))


def order_first():
    row, col = iotas(256, 256)
    return one_hot(((col & 3) * 64 + ((col >> 2) & 1) * 32 + (col >> 3)) == row)


def order_last():
    row, col = iotas(256, 256)
    x, y = (row >> 3) & 3, row >> 5
    return one_hot(((row & 3) * 64 + ((row >> 2) & 1) * 32 + x * 8 + y) == col)


def cycle_order():
    row, col = iotas(256, 256)
    r, x, y, zl, h = row & 1, (row >> 1) & 3, (row >> 3) & 7, (row >> 6) & 1, row >> 7
    return one_hot(r * 128 + zl * 64 + h * 32 + x * 8 + y == col)


def circle(steps):
    u = (steps + TURN // 8) & (TURN - 1)
    quad = u // (TURN // 4)
    t = ((u & (TURN // 4 - 1)) - TURN // 8).astype(F32) * (2.0 * math.pi / TURN)
    q = t * t
    sine = t * (1.0 + q * (-1 / 6 + q * (1 / 120 + q * (-1 / 5040 + q * (1 / 362880)))))
    cosine = 1.0 + q * (-1 / 2 + q * (1 / 24 + q * (-1 / 720 + q * (1 / 40320))))
    odd = (quad & 1) == 1
    cos = jnp.where(odd, sine, cosine)
    sin = jnp.where(odd, cosine, sine)
    cos = jnp.where((quad == 1) | (quad == 2), -cos, cos)
    return cos, jnp.where(quad >= 2, -sin, sin)


def ring_distance(d, n):
    return min(d, n - d)


Z_STEPS = sorted(range(1, NZ), key=lambda d: -ring_distance(d, NZ))
PLANE_STEPS = sorted(
    [(e, d) for e in range(NY) for d in range(NX) if e or d],
    key=lambda p: -(ring_distance(p[0], NY) + ring_distance(p[1], NX)),
)


def step_kernel(
    syn_scale,
    sky_hbm,
    prev_hbm,
    noise_hbm,
    mask_hbm,
    cycles_hbm,
    m_hbm,
    spectrum_hbm,
    leg_hbm,
    wiener_out,
    signal_out,
    sky,
    prev,
    noise,
    mask,
    cycles,
    m_ref,
    spectrum,
    blocks,
    table,
    phase_cos,
    phase_sin,
    part,
    leg,
    leg_p,
    core_buf,
    z_send,
    z_recv,
    p_send,
    p_recv,
    back,
    back_buf,
    q_send,
    q_recv,
    w_send,
    w_recv,
    modes,
    rotated,
    send_sem,
    recv_sem,
    load_sem,
):
    g, b, zh = lax.axis_index("grp"), lax.axis_index("blk"), lax.axis_index("real")
    x, y, zl = b % NX, (b // NX) % NY, b // PLANE
    z = zh * NZL + zl
    other = 1 - g
    ys = [(y + e) % NY for e in range(NY)]
    xs = [(x + d) % NX for d in range(NX)]

    core_peer = {"grp": other}
    z_peers = []
    for d in Z_STEPS:
        z_ = (z + d) % NZ
        z_peers.append((z_ % NZL, z_ // NZL, {"blk": (z_ % NZL) * PLANE + b % PLANE, "real": z_ // NZL}))
    plane_peers = [
        (ys[e] * NX + xs[d], {"blk": zl * PLANE + ys[e] * NX + xs[d]}) for e, d in PLANE_STEPS
    ]
    here = b % PLANE

    loads = [
        pltpu.make_async_copy(src, dst, load_sem.at[i])
        for i, (src, dst) in enumerate(
            [
                (m_hbm, m_ref),
                (cycles_hbm, cycles),
                (noise_hbm, noise),
                (mask_hbm, mask),
                (sky_hbm, sky),
                (prev_hbm, prev),
                (spectrum_hbm, spectrum),
                (leg_hbm, leg),
            ]
        )
    ]
    for load in loads:
        load.start()
    barrier = pltpu.get_barrier_semaphore()
    everyone = [core_peer] + [p[-1] for p in z_peers] + [p[-1] for p in plane_peers]
    for peer in everyone:
        pl.semaphore_signal(barrier, inc=1, device_id=peer, device_id_type=MESH)

    loads[0].wait()
    m = m_ref[...]
    fine_row = lax.broadcasted_iota(jnp.int32, (32, ORDERS), 0)
    row = lax.broadcasted_iota(jnp.int32, (16, ORDERS), 0)
    fine_cos, fine_sin = circle(m * fine_row * 2)
    coarse_cos, coarse_sin = circle(m * row * 64)
    for a in range(SPAN // 32):
        ca, sa = coarse_cos[a : a + 1], coarse_sin[a : a + 1]
        rows = slice(32 * a, 32 * (a + 1))
        table[rows, :ORDERS] = (ca * fine_cos - sa * fine_sin).astype(BF16)
        table[rows, ORDERS:] = (sa * fine_cos + ca * fine_sin).astype(BF16)
    loads[1].wait()
    parity = jnp.where((row & 1) == 1, cycles[:, 1:2], cycles[:, 0:1]) & 1
    pixel = g * (BLOCKS * SPAN) + (row >> 1) * SPAN
    pc, ps = circle(m * ((2 * pixel + parity) & (TURN - 1)))
    phase_cos[...] = pc
    phase_sin[...] = ps

    for load in loads[2:6]:
        load.wait()
    weight = mask[...].astype(F32) / (noise[...] - 0.5)
    of_prev = 2.0 / (weight + 2.0)
    of_sky = weight / (weight + 2.0)
    for i in range(64):
        tile, r = i // 2, i % 2
        at = pl.Slice(i, 16, 64)
        value = of_sky[i : i + 1] * sky[at, :] + of_prev[i : i + 1] * prev[at, :]
        q, t = tile // 4, tile % 4
        blocks[16 * (2 * q + r) : 16 * (2 * q + r + 1), 128 * t : 128 * (t + 1)] = value.astype(
            BF16
        )
    norm = (2 * BLOCKS * SPAN) ** -0.5
    for n in range(2):
        cols = slice(256 * n, 256 * (n + 1))
        sum_cos = dot_nn(blocks[...], table[:, 256 * n : 256 * (n + 1)])
        sum_sin = dot_nn(blocks[...], table[:, ORDERS + 256 * n : ORDERS + 256 * (n + 1)])
        for r in range(2):
            re = jnp.zeros((16, 256), F32)
            im = jnp.zeros((16, 256), F32)
            for q in range(BLOCKS):
                i = 2 * q + r
                c, s = pc[i : i + 1, cols], ps[i : i + 1, cols]
                yc, ys_ = sum_cos[16 * i : 16 * (i + 1)], sum_sin[16 * i : 16 * (i + 1)]
                re = re + (yc * c - ys_ * s)
                im = im - (ys_ * c + yc * s)
            part[r, 0, :, cols] = re * norm
            part[r, 1, :, cols] = im * norm

    pl.semaphore_wait(barrier, len(everyone))

    def send(phase, src, dst, peer):
        pltpu.make_async_remote_copy(
            src_ref=src,
            dst_ref=dst,
            send_sem=send_sem.at[phase],
            recv_sem=recv_sem.at[phase],
            device_id=peer,
            device_id_type=MESH,
        ).start()

    def keep(phase, src, dst):
        pltpu.make_async_copy(src, dst, recv_sem.at[phase]).start()

    def arrived(phase, ref):
        pltpu.make_async_copy(ref, ref, recv_sem.at[phase]).wait()

    def left(phase, ref):
        pltpu.make_async_copy(ref, ref, send_sem.at[phase]).wait()

    send(0, part.at[other], core_buf, core_peer)
    arrived(0, core_buf)
    for c in range(2):
        total = (part[g, c] + core_buf[c]).astype(BF16)
        for t in range(NZL):
            z_send[t, 16 * c : 16 * (c + 1)] = total[:, 128 * t : 128 * (t + 1)]
    for zl_, zh_, peer in z_peers:
        send(1, z_send.at[zl_], z_recv.at[2 * zl + zh], peer)
    keep(1, z_send.at[zl], z_recv.at[2 * zl + zh])
    loads[7].wait()
    permute = cycle_order()
    for s in range(4):
        leg_p[s] = dot_nn(leg[s], permute).astype(BF16)
    arrived(1, z_recv)
    gathered = z_recv[...].reshape(256, 128)
    turned = dot_nt(order_rows(0), gathered[:128]) + dot_nt(order_rows(1), gathered[128:])
    p_send[...] = turned.astype(BF16).reshape(PLANE, 8, 128)
    slot = x * NY + y
    for i, peer in plane_peers:
        send(2, p_send.at[i], p_recv.at[g, slot], peer)
    keep(2, p_send.at[here], p_recv.at[g, slot])
    arrived(2, p_recv.at[g])
    send(3, p_recv.at[g], p_recv.at[g], core_peer)
    arrived(3, p_recv.at[other])

    first = order_first()
    columns = [
        dot_nn(first, p_recv[r].reshape(256, 128)).T for r in range(2)
    ]
    loads[6].wait()
    power = spectrum[...]
    scale = power / (power + 0.5)
    for s in range(4):
        rows = jnp.concatenate(
            [
                columns[r][64 * t : 64 * (t + 1), 64 * s : 64 * (s + 1)]
                for r in range(2)
                for t in range(2)
            ],
            axis=1,
        ).astype(BF16)
        wiener = dot_nt(rows, leg_p[s]) * scale
        for p in range(4):
            for t in range(8):
                wiener_out[pl.Slice((p // 2) * 1024 + (p % 2) * 32 + t * 4 + s, 16, 64), :] = wiener[
                    16 * p : 16 * (p + 1), 128 * t : 128 * (t + 1)
                ]
        partial = dot_nn(wiener.astype(BF16), leg_p[s]) * syn_scale
        back[0, s] = partial[:, :128]
        back[1, s] = partial[:, 128:]

    send(4, back.at[other], back_buf, core_peer)
    arrived(4, back_buf)
    both = back[g] + back_buf[...]
    halves = [
        jnp.concatenate([both[s][:, 64 * t : 64 * (t + 1)] for s in range(4)], axis=1)
        for t in range(2)
    ]
    turned = jnp.concatenate(halves, axis=0).T.astype(BF16)
    q_send[...] = dot_nn(order_last(), turned).astype(BF16).reshape(PLANE, 8, 128)
    for i, peer in plane_peers:
        send(5, q_send.at[i], q_recv.at[here], peer)
    keep(5, q_send.at[here], q_recv.at[here])
    arrived(5, q_recv)
    plane = q_recv[...].reshape(256, 128)
    for h in range(2):
        turned = dot_nn(order_cols(h), plane).T.astype(BF16)
        w_send[4 * h : 4 * h + 4] = turned.reshape(4, 32, 128)
    for zl_, zh_, peer in z_peers:
        send(6, w_send.at[2 * zl_ + zh_], w_recv.at[2 * zl + zh], peer)
    keep(6, w_send.at[2 * zl + zh], w_recv.at[2 * zl + zh])
    arrived(6, w_recv)
    for t in range(NZL):
        modes[g, :, 128 * t : 128 * (t + 1)] = (
            w_recv[2 * t].astype(F32) + w_recv[2 * t + 1].astype(F32)
        ).astype(BF16)
    send(7, modes.at[g], modes.at[g], core_peer)
    arrived(7, modes.at[other])

    for r in range(2):
        re, im = modes[r, :16].astype(F32), modes[r, 16:].astype(F32)
        for q in range(BLOCKS):
            i = 2 * q + r
            c, s = phase_cos[i : i + 1], phase_sin[i : i + 1]
            rotated[16 * i : 16 * (i + 1), :ORDERS] = (re * c - im * s).astype(BF16)
            rotated[16 * i : 16 * (i + 1), ORDERS:] = (-(im * c + re * s)).astype(BF16)
    for n in range(2):
        pixels = dot_nt(rotated[...], table[256 * n : 256 * (n + 1)]) * ORDERS**-0.5
        for i in range(2 * BLOCKS):
            for t in range(2):
                start = ((i // 2) * 4 + 2 * n + t) * 2 + i % 2
                signal_out[pl.Slice(start, 16, 64), :] = pixels[
                    16 * i : 16 * (i + 1), 128 * t : 128 * (t + 1)
                ]

    left(0, core_buf)
    left(1, z_recv.at[0:7])
    left(2, p_recv.at[0, 0:31])
    left(3, p_recv.at[0])
    left(4, back_buf)
    left(5, q_recv.at[0:31])
    left(6, w_recv.at[0:7])
    left(7, modes.at[0])


def step(inputs, syn_scale):
    def vmem(shape, dtype=BF16):
        return pltpu.VMEM(shape, dtype)

    block = pl.BlockSpec(memory_space=pltpu.VMEM)
    return pl.pallas_call(
        lambda *refs: step_kernel(syn_scale, *refs),
        out_shape=(
            jax.ShapeDtypeStruct((2048, 128), F32),
            jax.ShapeDtypeStruct((1024, 128), F32),
        ),
        in_specs=[pl.BlockSpec(memory_space=pltpu.HBM)] * 8,
        out_specs=(block, block),
        scratch_shapes=[
            vmem((1024, 128), F32),
            vmem((1024, 128), F32),
            vmem((64, 128), F32),
            vmem((64, 128), jnp.int32),
            vmem((1, 2), jnp.int32),
            vmem((1, ORDERS), jnp.int32),
            vmem((1, 1024), F32),
            vmem((32 * BLOCKS, SPAN)),
            vmem((SPAN, 2 * ORDERS)),
            vmem((16, ORDERS), F32),
            vmem((16, ORDERS), F32),
            vmem((2, 2, 16, ORDERS), F32),
            vmem((4, 1024, 256)),
            vmem((4, 1024, 256)),
            vmem((2, 16, ORDERS), F32),
            vmem((NZL, 32, 128)),
            vmem((NZ, 32, 128)),
            vmem((PLANE, 8, 128)),
            vmem((2, PLANE, 8, 128)),
            vmem((2, 4, 64, 128), F32),
            vmem((4, 64, 128), F32),
            vmem((PLANE, 8, 128)),
            vmem((PLANE, 8, 128)),
            vmem((NZ, 32, 128)),
            vmem((NZ, 32, 128)),
            vmem((2, 32, ORDERS)),
            vmem((32 * BLOCKS, 2 * ORDERS)),
            pltpu.SemaphoreType.DMA((8,)),
            pltpu.SemaphoreType.DMA((8,)),
            pltpu.SemaphoreType.DMA((8,)),
        ],
        compiler_params=pltpu.CompilerParams(
            collective_id=0, has_side_effects=True, vmem_limit_bytes=67043328
        ),
    )(*inputs)


def per_device(
    sky_data, signal_prev, noise_var, mask_flags, cycle_table, m_table, spectrum, legendre
):
    half_len = sky_data.shape[2]
    total_l = legendre.shape[1] * lax.axis_size("grp") * lax.axis_size("real")
    syn_scale = (legendre.shape[2] / total_l) ** 0.5

    def rows(a):
        return a.reshape(-1, 2, half_len // 128, 128).swapaxes(1, 2).reshape(-1, 128)

    inputs = (
        rows(sky_data),
        rows(signal_prev),
        rows(noise_var),
        rows(mask_flags),
        cycle_table[None],
        m_table[None],
        spectrum[None],
        legendre,
    )
    wiener, signal = step(inputs, syn_scale)
    wiener_alm = (
        wiener.reshape(32, 2, 8, 4, 128).transpose(0, 1, 3, 2, 4).reshape(32, 2, 4, 1024)
    )
    signal_next = signal.reshape(16, 32, 2, 128).transpose(0, 2, 1, 3).reshape(16, 2, half_len)
    return (wiener_alm, signal_next)


def solution(mesh):
    in_specs = (
        P("real", "blk", "grp"),
        P("real", "blk", "grp"),
        P("blk", "grp"),
        P("blk", "grp"),
        P("blk"),
        P(),
        P(("grp", "real")),
        P("blk", ("grp", "real"), None),
    )
    out_specs = (P(None, None, "blk", ("grp", "real")), P("real", "blk", "grp"))
    return jax.shard_map(
        per_device, mesh=mesh, in_specs=in_specs, out_specs=out_specs, check_vma=False
    )
```

```python
import math

import jax
import jax.numpy as jnp
from jax import lax
from jax.experimental import pallas as pl
from jax.experimental.pallas import tpu as pltpu
from jax.sharding import PartitionSpec as P


NX, NY, NZ = 4, 8, 8
NZL = 4
PLANE = NX * NY
BLOCKS = 8
SPAN = 512
ORDERS = 512
TURN = 16384
MESH = pl.DeviceIdType.MESH
F32 = jnp.float32
BF16 = jnp.bfloat16


def dot_nn(a, b):
    return jnp.dot(a, b, preferred_element_type=F32)


def dot_nt(a, b):
    return lax.dot_general(a, b, (((1,), (1,)), ((), ())), preferred_element_type=F32)


def iotas(rows, cols):
    row = lax.broadcasted_iota(jnp.int32, (rows, cols), 0)
    col = lax.broadcasted_iota(jnp.int32, (rows, cols), 1)
    return row, col


def one_hot(match):
    return jnp.where(match, 1.0, 0.0).astype(BF16)


def order_rows(h):
    row, col = iotas(256, 128)
    return one_hot(((row >> 3) * 4 + (row & 3) == col) & (((row >> 2) & 1) == h))


def order_cols(h):
    row, col = iotas(128, 256)
    return one_hot(((col >> 3) * 4 + (col & 3) == row) & (((col >> 2) & 1) == h))


def order_first():
    row, col = iotas(256, 256)
    return one_hot(((col & 3) * 64 + ((col >> 2) & 1) * 32 + (col >> 3)) == row)


def order_last():
    row, col = iotas(256, 256)
    x, y = (row >> 3) & 3, row >> 5
    return one_hot(((row & 3) * 64 + ((row >> 2) & 1) * 32 + x * 8 + y) == col)


def cycle_order():
    row, col = iotas(256, 256)
    r, x, y, zl, h = row & 1, (row >> 1) & 3, (row >> 3) & 7, (row >> 6) & 1, row >> 7
    return one_hot(r * 128 + zl * 64 + h * 32 + x * 8 + y == col)


def circle(steps):
    u = (steps + TURN // 8) & (TURN - 1)
    quad = u // (TURN // 4)
    t = ((u & (TURN // 4 - 1)) - TURN // 8).astype(F32) * (2.0 * math.pi / TURN)
    q = t * t
    sine = t * (1.0 + q * (-1 / 6 + q * (1 / 120 + q * (-1 / 5040 + q * (1 / 362880)))))
    cosine = 1.0 + q * (-1 / 2 + q * (1 / 24 + q * (-1 / 720 + q * (1 / 40320))))
    odd = (quad & 1) == 1
    cos = jnp.where(odd, sine, cosine)
    sin = jnp.where(odd, cosine, sine)
    cos = jnp.where((quad == 1) | (quad == 2), -cos, cos)
    return cos, jnp.where(quad >= 2, -sin, sin)


def ring_distance(d, n):
    return min(d, n - d)


Z_STEPS = sorted(range(1, NZ), key=lambda d: -ring_distance(d, NZ))
PLANE_STEPS = sorted(
    [(e, d) for e in range(NY) for d in range(NX) if e or d],
    key=lambda p: -(ring_distance(p[0], NY) + ring_distance(p[1], NX)),
)


def step_kernel(
    syn_scale,
    sky_hbm,
    prev_hbm,
    noise_hbm,
    mask_hbm,
    cycles_hbm,
    m_hbm,
    spectrum_hbm,
    leg_hbm,
    wiener_out,
    signal_out,
    sky,
    prev,
    noise,
    mask,
    cycles,
    m_ref,
    spectrum,
    blocks,
    table,
    phase_cos,
    phase_sin,
    part,
    leg,
    leg_p,
    core_buf,
    z_send,
    z_recv,
    p_send,
    p_recv,
    back,
    back_buf,
    q_send,
    q_recv,
    w_send,
    w_recv,
    modes,
    rotated,
    wiener_rows,
    picks,
    send_sem,
    recv_sem,
    load_sem,
):
    g, b, zh = lax.axis_index("grp"), lax.axis_index("blk"), lax.axis_index("real")
    x, y, zl = b % NX, (b // NX) % NY, b // PLANE
    z = zh * NZL + zl
    other = 1 - g
    ys = [(y + e) % NY for e in range(NY)]
    xs = [(x + d) % NX for d in range(NX)]

    core_peer = {"grp": other}
    z_peers = []
    for d in Z_STEPS:
        z_ = (z + d) % NZ
        z_peers.append((z_ % NZL, z_ // NZL, {"blk": (z_ % NZL) * PLANE + b % PLANE, "real": z_ // NZL}))
    plane_peers = [
        (ys[e] * NX + xs[d], {"blk": zl * PLANE + ys[e] * NX + xs[d]}) for e, d in PLANE_STEPS
    ]
    here = b % PLANE

    barrier = pltpu.get_barrier_semaphore()
    everyone = [p[-1] for p in plane_peers] + [p[-1] for p in z_peers]
    everyone += [{"grp": other, **p[-1]} for p in z_peers] + [core_peer]
    for peer in everyone:
        pl.semaphore_signal(barrier, inc=1, device_id=peer, device_id_type=MESH)

    loads = [
        pltpu.make_async_copy(src, dst, load_sem.at[i])
        for i, (src, dst) in enumerate(
            [
                (m_hbm, m_ref),
                (cycles_hbm, cycles),
                (noise_hbm, noise),
                (mask_hbm, mask),
                (sky_hbm, sky),
                (prev_hbm, prev),
                (spectrum_hbm, spectrum),
                (leg_hbm, leg),
            ]
        )
    ]
    for load in loads:
        load.start()

    loads[0].wait()
    m = m_ref[...]
    fine_row = lax.broadcasted_iota(jnp.int32, (32, ORDERS), 0)
    row = lax.broadcasted_iota(jnp.int32, (16, ORDERS), 0)
    fine_cos, fine_sin = circle(m * fine_row * 2)
    coarse_cos, coarse_sin = circle(m * row * 64)
    for a in range(SPAN // 32):
        ca, sa = coarse_cos[a : a + 1], coarse_sin[a : a + 1]
        rows = slice(32 * a, 32 * (a + 1))
        table[rows, :ORDERS] = (ca * fine_cos - sa * fine_sin).astype(BF16)
        table[rows, ORDERS:] = (sa * fine_cos + ca * fine_sin).astype(BF16)
    loads[1].wait()
    parity = jnp.where((row & 1) == 1, cycles[:, 1:2], cycles[:, 0:1]) & 1
    pixel = g * (BLOCKS * SPAN) + (row >> 1) * SPAN
    pc, ps = circle(m * ((2 * pixel + parity) & (TURN - 1)))
    phase_cos[...] = pc
    phase_sin[...] = ps

    for load in loads[2:6]:
        load.wait()
    weight = mask[...].astype(F32) / (noise[...] - 0.5)
    of_prev = 2.0 / (weight + 2.0)
    of_sky = weight / (weight + 2.0)
    for i in range(64):
        tile, r = i // 2, i % 2
        at = pl.Slice(i, 16, 64)
        value = of_sky[i : i + 1] * sky[at, :] + of_prev[i : i + 1] * prev[at, :]
        q, t = tile // 4, tile % 4
        blocks[16 * (2 * q + r) : 16 * (2 * q + r + 1), 128 * t : 128 * (t + 1)] = value.astype(
            BF16
        )
    norm = (2 * BLOCKS * SPAN) ** -0.5
    for n in range(2):
        cols = slice(256 * n, 256 * (n + 1))
        sum_cos = dot_nn(blocks[...], table[:, 256 * n : 256 * (n + 1)])
        sum_sin = dot_nn(blocks[...], table[:, ORDERS + 256 * n : ORDERS + 256 * (n + 1)])
        for r in range(2):
            re = jnp.zeros((16, 256), F32)
            im = jnp.zeros((16, 256), F32)
            for q in range(BLOCKS):
                i = 2 * q + r
                c, s = pc[i : i + 1, cols], ps[i : i + 1, cols]
                yc, ys_ = sum_cos[16 * i : 16 * (i + 1)], sum_sin[16 * i : 16 * (i + 1)]
                re = re + (yc * c - ys_ * s)
                im = im - (ys_ * c + yc * s)
            part[r, 0, :, cols] = re * norm
            part[r, 1, :, cols] = im * norm

    pl.semaphore_wait(barrier, len(everyone))

    def send(phase, src, dst, peer):
        pltpu.make_async_remote_copy(
            src_ref=src,
            dst_ref=dst,
            send_sem=send_sem.at[phase],
            recv_sem=recv_sem.at[phase],
            device_id=peer,
            device_id_type=MESH,
        ).start()

    def keep(phase, src, dst):
        pltpu.make_async_copy(src, dst, recv_sem.at[phase]).start()

    def arrived(phase, ref):
        pltpu.make_async_copy(ref, ref, recv_sem.at[phase]).wait()

    def left(phase, ref):
        pltpu.make_async_copy(ref, ref, send_sem.at[phase]).wait()

    send(0, part.at[other], core_buf, core_peer)
    arrived(0, core_buf)
    for c in range(2):
        total = (part[g, c] + core_buf[c]).astype(BF16)
        for t in range(NZL):
            z_send[t, 16 * c : 16 * (c + 1)] = total[:, 128 * t : 128 * (t + 1)]
    for zl_, zh_, peer in z_peers:
        send(1, z_send.at[zl_], z_recv.at[2 * zl + zh], peer)
    keep(1, z_send.at[zl], z_recv.at[2 * zl + zh])
    for h in range(2):
        picks[h, :, :128] = order_rows(h)
    loads[7].wait()
    permute = cycle_order()
    for s in range(4):
        leg_p[s] = dot_nn(leg[s], permute).astype(BF16)
    picks[2] = order_first()
    picks[3] = order_last()
    for h in range(2):
        picks[4 + h, :128] = order_cols(h)
    arrived(1, z_recv)
    gathered = z_recv[...].reshape(256, 128)
    turned = dot_nt(picks[0, :, :128], gathered[:128]) + dot_nt(
        picks[1, :, :128], gathered[128:]
    )
    p_send[...] = turned.astype(BF16).reshape(PLANE, 8, 128)
    slot = x * NY + y
    for i, peer in plane_peers:
        send(2, p_send.at[i], p_recv.at[g, slot], peer)
    keep(2, p_send.at[here], p_recv.at[g, slot])
    arrived(2, p_recv.at[g])
    send(3, p_recv.at[g], p_recv.at[g], core_peer)
    arrived(3, p_recv.at[other])

    first = picks[2]
    columns = [
        dot_nn(first, p_recv[r].reshape(256, 128)).T for r in range(2)
    ]
    loads[6].wait()
    power = spectrum[...]
    scale = power / (power + 0.5)
    for s in range(4):
        rows = jnp.concatenate(
            [
                columns[r][64 * t : 64 * (t + 1), 64 * s : 64 * (s + 1)]
                for r in range(2)
                for t in range(2)
            ],
            axis=1,
        ).astype(BF16)
        wiener = dot_nt(rows, leg_p[s]) * scale
        wiener_rows[s] = wiener
        partial = dot_nn(wiener.astype(BF16), leg_p[s]) * syn_scale
        back[0, s] = partial[:, :128]
        back[1, s] = partial[:, 128:]
        send(4, back.at[other, s], back_buf.at[s], core_peer)

    arrived(4, back_buf)
    both = back[g] + back_buf[...]
    halves = [
        jnp.concatenate([both[s][:, 64 * t : 64 * (t + 1)] for s in range(4)], axis=1)
        for t in range(2)
    ]
    turned = jnp.concatenate(halves, axis=0).T.astype(BF16)
    q_send[...] = dot_nn(picks[3], turned).astype(BF16).reshape(PLANE, 8, 128)
    for i, peer in plane_peers:
        send(5, q_send.at[i], q_recv.at[here], peer)
    keep(5, q_send.at[here], q_recv.at[here])
    for s in range(4):
        for p in range(4):
            for t in range(8):
                start = (p // 2) * 1024 + (p % 2) * 32 + t * 4 + s
                wiener_out[pl.Slice(start, 16, 64), :] = wiener_rows[
                    s, 16 * p : 16 * (p + 1), 128 * t : 128 * (t + 1)
                ]
    arrived(5, q_recv)
    plane = q_recv[...].reshape(256, 128)
    for h in range(2):
        turned = dot_nn(picks[4 + h, :128], plane).T.astype(BF16)
        w_send[4 * h : 4 * h + 4] = turned.reshape(4, 32, 128)
    mine = 2 * zl + zh
    for zl_, zh_, peer in z_peers:
        for core in (other, g):
            send(6, w_send.at[2 * zl_ + zh_], w_recv.at[g, mine], {"grp": core, **peer})
    send(6, w_send.at[mine], w_recv.at[g, mine], core_peer)
    keep(6, w_send.at[mine], w_recv.at[g, mine])
    arrived(6, w_recv)
    for r in range(2):
        for t in range(NZL):
            modes[r, :, 128 * t : 128 * (t + 1)] = (
                w_recv[r, 2 * t].astype(F32) + w_recv[r, 2 * t + 1].astype(F32)
            ).astype(BF16)

    for r in range(2):
        re, im = modes[r, :16].astype(F32), modes[r, 16:].astype(F32)
        for q in range(BLOCKS):
            i = 2 * q + r
            c, s = phase_cos[i : i + 1], phase_sin[i : i + 1]
            rotated[16 * i : 16 * (i + 1), :ORDERS] = (re * c - im * s).astype(BF16)
            rotated[16 * i : 16 * (i + 1), ORDERS:] = (-(im * c + re * s)).astype(BF16)
    for n in range(2):
        pixels = dot_nt(rotated[...], table[256 * n : 256 * (n + 1)]) * ORDERS**-0.5
        for i in range(2 * BLOCKS):
            for t in range(2):
                start = ((i // 2) * 4 + 2 * n + t) * 2 + i % 2
                signal_out[pl.Slice(start, 16, 64), :] = pixels[
                    16 * i : 16 * (i + 1), 128 * t : 128 * (t + 1)
                ]

    left(0, core_buf)
    left(1, z_recv.at[0:7])
    left(2, p_recv.at[0, 0:31])
    left(3, p_recv.at[0])
    left(4, back_buf)
    left(5, q_recv.at[0:31])
    left(6, w_recv.at[0])
    left(6, w_recv.at[0, 0:7])


def store_kernel(wiener, signal, wiener_out, signal_out, sem):
    copies = []
    for i, rows in enumerate([pl.ds(512 * n, 512) for n in range(4)]):
        copies.append(pltpu.make_async_copy(wiener.at[rows], wiener_out.at[rows], sem.at[i]))
        if i < 2:
            copies.append(
                pltpu.make_async_copy(signal.at[rows], signal_out.at[rows], sem.at[4 + i])
            )
    for copy in copies:
        copy.start()
    for copy in copies:
        copy.wait()


def store(wiener, signal):
    hbm = pl.BlockSpec(memory_space=pltpu.HBM)
    block = pl.BlockSpec(memory_space=pltpu.VMEM)
    return pl.pallas_call(
        store_kernel,
        out_shape=(
            jax.ShapeDtypeStruct((2048, 128), F32),
            jax.ShapeDtypeStruct((1024, 128), F32),
        ),
        in_specs=[block] * 2,
        out_specs=(hbm, hbm),
        scratch_shapes=[pltpu.SemaphoreType.DMA((6,))],
        compiler_params=pltpu.CompilerParams(vmem_limit_bytes=16 * 1024 * 1024),
    )(wiener, signal)


def step(inputs, syn_scale):
    def vmem(shape, dtype=BF16):
        return pltpu.VMEM(shape, dtype)

    block = pl.BlockSpec(memory_space=pltpu.VMEM)
    return pl.pallas_call(
        lambda *refs: step_kernel(syn_scale, *refs),
        out_shape=(
            jax.ShapeDtypeStruct((2048, 128), F32),
            jax.ShapeDtypeStruct((1024, 128), F32),
        ),
        in_specs=[pl.BlockSpec(memory_space=pltpu.HBM)] * 8,
        out_specs=(block, block),
        scratch_shapes=[
            vmem((1024, 128), F32),
            vmem((1024, 128), F32),
            vmem((64, 128), F32),
            vmem((64, 128), jnp.int32),
            vmem((1, 2), jnp.int32),
            vmem((1, ORDERS), jnp.int32),
            vmem((1, 1024), F32),
            vmem((32 * BLOCKS, SPAN)),
            vmem((SPAN, 2 * ORDERS)),
            vmem((16, ORDERS), F32),
            vmem((16, ORDERS), F32),
            vmem((2, 2, 16, ORDERS), F32),
            vmem((4, 1024, 256)),
            vmem((4, 1024, 256)),
            vmem((2, 16, ORDERS), F32),
            vmem((NZL, 32, 128)),
            vmem((NZ, 32, 128)),
            vmem((PLANE, 8, 128)),
            vmem((2, PLANE, 8, 128)),
            vmem((2, 4, 64, 128), F32),
            vmem((4, 64, 128), F32),
            vmem((PLANE, 8, 128)),
            vmem((PLANE, 8, 128)),
            vmem((NZ, 32, 128)),
            vmem((2, NZ, 32, 128)),
            vmem((2, 32, ORDERS)),
            vmem((32 * BLOCKS, 2 * ORDERS)),
            vmem((4, 64, 1024), F32),
            vmem((6, 256, 256)),
            pltpu.SemaphoreType.DMA((7,)),
            pltpu.SemaphoreType.DMA((7,)),
            pltpu.SemaphoreType.DMA((8,)),
        ],
        compiler_params=pltpu.CompilerParams(
            collective_id=0, has_side_effects=True, vmem_limit_bytes=40000000
        ),
    )(*[pltpu.with_memory_space_constraint(a, pltpu.HBM) for a in inputs])


def per_device(
    sky_data, signal_prev, noise_var, mask_flags, cycle_table, m_table, spectrum, legendre
):
    half_len = sky_data.shape[2]
    total_l = legendre.shape[1] * lax.axis_size("grp") * lax.axis_size("real")
    syn_scale = (legendre.shape[2] / total_l) ** 0.5

    def rows(a):
        return a.reshape(-1, 2, half_len // 128, 128).swapaxes(1, 2).reshape(-1, 128)

    inputs = (
        rows(sky_data),
        rows(signal_prev),
        rows(noise_var),
        rows(mask_flags),
        cycle_table[None],
        m_table[None],
        spectrum[None],
        legendre,
    )
    wiener, signal = store(*step(inputs, syn_scale))
    wiener_alm = (
        wiener.reshape(32, 2, 8, 4, 128).transpose(0, 1, 3, 2, 4).reshape(32, 2, 4, 1024)
    )
    signal_next = signal.reshape(16, 32, 2, 128).transpose(0, 2, 1, 3).reshape(16, 2, half_len)
    return (wiener_alm, signal_next)


def solution(mesh):
    in_specs = (
        P("real", "blk", "grp"),
        P("real", "blk", "grp"),
        P("blk", "grp"),
        P("blk", "grp"),
        P("blk"),
        P(),
        P(("grp", "real")),
        P("blk", ("grp", "real"), None),
    )
    out_specs = (P(None, None, "blk", ("grp", "real")), P("real", "blk", "grp"))
    return jax.shard_map(
        per_device, mesh=mesh, in_specs=in_specs, out_specs=out_specs, check_vma=False
    )
```

```python
import math

import jax
import jax.numpy as jnp
from jax import lax
from jax.experimental import pallas as pl
from jax.experimental.pallas import tpu as pltpu
from jax.sharding import PartitionSpec as P


NX, NY, NZ = 4, 8, 8
NZL = 4
PLANE = NX * NY
BLOCKS = 8
SPAN = 512
ORDERS = 512
TURN = 16384
MESH = pl.DeviceIdType.MESH
F32 = jnp.float32
BF16 = jnp.bfloat16


def dot_nn(a, b):
    return jnp.dot(a, b, preferred_element_type=F32)


def dot_nt(a, b):
    return lax.dot_general(a, b, (((1,), (1,)), ((), ())), preferred_element_type=F32)


def iotas(rows, cols):
    row = lax.broadcasted_iota(jnp.int32, (rows, cols), 0)
    col = lax.broadcasted_iota(jnp.int32, (rows, cols), 1)
    return row, col


def one_hot(match):
    return jnp.where(match, 1.0, 0.0).astype(BF16)


def order_rows(h):
    row, col = iotas(256, 128)
    return one_hot(((row >> 3) * 4 + (row & 3) == col) & (((row >> 2) & 1) == h))


def order_cols(h):
    row, col = iotas(128, 256)
    return one_hot(((col >> 3) * 4 + (col & 3) == row) & (((col >> 2) & 1) == h))


def order_first():
    row, col = iotas(256, 256)
    return one_hot(((col & 3) * 64 + ((col >> 2) & 1) * 32 + (col >> 3)) == row)


def order_last():
    row, col = iotas(256, 256)
    x, y = (row >> 3) & 3, row >> 5
    return one_hot(((row & 3) * 64 + ((row >> 2) & 1) * 32 + x * 8 + y) == col)


def cycle_order():
    row, col = iotas(256, 256)
    r, x, y, zl, h = row & 1, (row >> 1) & 3, (row >> 3) & 7, (row >> 6) & 1, row >> 7
    return one_hot(r * 128 + zl * 64 + h * 32 + x * 8 + y == col)


def circle(steps):
    u = (steps + TURN // 8) & (TURN - 1)
    quad = u // (TURN // 4)
    t = ((u & (TURN // 4 - 1)) - TURN // 8).astype(F32) * (2.0 * math.pi / TURN)
    q = t * t
    sine = t * (1.0 + q * (-1 / 6 + q * (1 / 120 + q * (-1 / 5040 + q * (1 / 362880)))))
    cosine = 1.0 + q * (-1 / 2 + q * (1 / 24 + q * (-1 / 720 + q * (1 / 40320))))
    odd = (quad & 1) == 1
    cos = jnp.where(odd, sine, cosine)
    sin = jnp.where(odd, cosine, sine)
    cos = jnp.where((quad == 1) | (quad == 2), -cos, cos)
    return cos, jnp.where(quad >= 2, -sin, sin)


def ring_distance(d, n):
    return min(d, n - d)


Z_STEPS = sorted(range(1, NZ), key=lambda d: -ring_distance(d, NZ))
PLANE_STEPS = sorted(
    [(e, d) for e in range(NY) for d in range(NX) if e or d],
    key=lambda p: -(ring_distance(p[0], NY) + ring_distance(p[1], NX)),
)


def step_kernel(
    syn_scale,
    sky_hbm,
    prev_hbm,
    noise_hbm,
    mask_hbm,
    cycles_hbm,
    m_hbm,
    spectrum_hbm,
    leg_hbm,
    wiener_out,
    signal_out,
    sky,
    prev,
    noise,
    mask,
    cycles,
    m_ref,
    spectrum,
    blocks,
    table,
    phase_cos,
    phase_sin,
    part,
    leg,
    leg_p,
    z_send,
    z_recv,
    p_send,
    p_recv,
    back,
    back_buf,
    q_send,
    q_recv,
    w_send,
    w_recv,
    modes,
    rotated,
    wiener_rows,
    picks,
    send_sem,
    recv_sem,
    load_sem,
):
    g, b, zh = lax.axis_index("grp"), lax.axis_index("blk"), lax.axis_index("real")
    x, y, zl = b % NX, (b // NX) % NY, b // PLANE
    z = zh * NZL + zl
    other = 1 - g
    ys = [(y + e) % NY for e in range(NY)]
    xs = [(x + d) % NX for d in range(NX)]

    core_peer = {"grp": other}
    z_peers = []
    for d in Z_STEPS:
        z_ = (z + d) % NZ
        z_peers.append((z_ % NZL, z_ // NZL, {"blk": (z_ % NZL) * PLANE + b % PLANE, "real": z_ // NZL}))
    plane_peers = [
        (ys[e] * NX + xs[d], {"blk": zl * PLANE + ys[e] * NX + xs[d]}) for e, d in PLANE_STEPS
    ]
    here = b % PLANE

    barrier = pltpu.get_barrier_semaphore()
    everyone = [p[-1] for p in plane_peers] + [p[-1] for p in z_peers]
    everyone += [{"grp": other, **p[-1]} for p in z_peers] + [core_peer]
    for peer in everyone:
        pl.semaphore_signal(barrier, inc=1, device_id=peer, device_id_type=MESH)

    loads = [
        pltpu.make_async_copy(src, dst, load_sem.at[i])
        for i, (src, dst) in enumerate(
            [
                (m_hbm, m_ref),
                (cycles_hbm, cycles),
                (noise_hbm, noise),
                (mask_hbm, mask),
                (sky_hbm, sky),
                (prev_hbm, prev),
                (spectrum_hbm, spectrum),
                (leg_hbm, leg),
            ]
        )
    ]
    for load in loads:
        load.start()

    loads[0].wait()
    m = m_ref[...]
    fine_row = lax.broadcasted_iota(jnp.int32, (32, ORDERS), 0)
    row = lax.broadcasted_iota(jnp.int32, (16, ORDERS), 0)
    fine_cos, fine_sin = circle(m * fine_row * 2)
    coarse_cos, coarse_sin = circle(m * row * 64)
    for a in range(SPAN // 32):
        ca, sa = coarse_cos[a : a + 1], coarse_sin[a : a + 1]
        rows = slice(32 * a, 32 * (a + 1))
        table[rows, :ORDERS] = (ca * fine_cos - sa * fine_sin).astype(BF16)
        table[rows, ORDERS:] = (sa * fine_cos + ca * fine_sin).astype(BF16)
    loads[1].wait()
    parity = jnp.where((row & 1) == 1, cycles[:, 1:2], cycles[:, 0:1]) & 1
    pixel = g * (BLOCKS * SPAN) + (row >> 1) * SPAN
    pc, ps = circle(m * ((2 * pixel + parity) & (TURN - 1)))
    phase_cos[...] = pc
    phase_sin[...] = ps

    for load in loads[2:6]:
        load.wait()
    weight = mask[...].astype(F32) / (noise[...] - 0.5)
    of_prev = 2.0 / (weight + 2.0)
    of_sky = weight / (weight + 2.0)
    for i in range(64):
        tile, r = i // 2, i % 2
        at = pl.Slice(i, 16, 64)
        value = of_sky[i : i + 1] * sky[at, :] + of_prev[i : i + 1] * prev[at, :]
        q, t = tile // 4, tile % 4
        blocks[16 * (2 * q + r) : 16 * (2 * q + r + 1), 128 * t : 128 * (t + 1)] = value.astype(
            BF16
        )
    norm = (2 * BLOCKS * SPAN) ** -0.5
    for n in range(2):
        cols = slice(256 * n, 256 * (n + 1))
        sum_cos = dot_nn(blocks[...], table[:, 256 * n : 256 * (n + 1)])
        sum_sin = dot_nn(blocks[...], table[:, ORDERS + 256 * n : ORDERS + 256 * (n + 1)])
        for r in range(2):
            re = jnp.zeros((16, 256), F32)
            im = jnp.zeros((16, 256), F32)
            for q in range(BLOCKS):
                i = 2 * q + r
                c, s = pc[i : i + 1, cols], ps[i : i + 1, cols]
                yc, ys_ = sum_cos[16 * i : 16 * (i + 1)], sum_sin[16 * i : 16 * (i + 1)]
                re = re + (yc * c - ys_ * s)
                im = im - (ys_ * c + yc * s)
            part[r, 0, :, cols] = re * norm
            part[r, 1, :, cols] = im * norm

    pl.semaphore_wait(barrier, len(everyone))

    def send(phase, src, dst, peer):
        pltpu.make_async_remote_copy(
            src_ref=src,
            dst_ref=dst,
            send_sem=send_sem.at[phase],
            recv_sem=recv_sem.at[phase],
            device_id=peer,
            device_id_type=MESH,
        ).start()

    def keep(phase, src, dst):
        pltpu.make_async_copy(src, dst, recv_sem.at[phase]).start()

    def arrived(phase, ref):
        pltpu.make_async_copy(ref, ref, recv_sem.at[phase]).wait()

    def left(phase, ref):
        pltpu.make_async_copy(ref, ref, send_sem.at[phase]).wait()

    for r in range(2):
        for c in range(2):
            half = part[r, c].astype(BF16)
            for t in range(NZL):
                z_send[r, t, 16 * c : 16 * (c + 1)] = half[:, 128 * t : 128 * (t + 1)]
    mine = 2 * zl + zh
    for zl_, zh_, peer in z_peers:
        for core in (other, g):
            send(1, z_send.at[core, zl_], z_recv.at[g, mine], {"grp": core, **peer})
    send(1, z_send.at[other, zl], z_recv.at[g, mine], core_peer)
    keep(1, z_send.at[g, zl], z_recv.at[g, mine])
    for h in range(2):
        picks[h, :, :128] = order_rows(h)
    loads[7].wait()
    permute = cycle_order()
    for s in range(4):
        leg_p[s] = dot_nn(leg[s], permute).astype(BF16)
    picks[2] = order_first()
    picks[3] = order_last()
    for h in range(2):
        picks[4 + h, :128] = order_cols(h)
    arrived(1, z_recv)
    gathered = z_recv[0].reshape(256, 128).astype(F32) + z_recv[1].reshape(256, 128).astype(F32)
    gathered = gathered.astype(BF16)
    turned = dot_nt(picks[0, :, :128], gathered[:128]) + dot_nt(
        picks[1, :, :128], gathered[128:]
    )
    p_send[...] = turned.astype(BF16).reshape(PLANE, 8, 128)
    slot = x * NY + y
    for i, peer in plane_peers:
        send(2, p_send.at[i], p_recv.at[g, slot], peer)
    keep(2, p_send.at[here], p_recv.at[g, slot])
    arrived(2, p_recv.at[g])
    send(3, p_recv.at[g], p_recv.at[g], core_peer)
    arrived(3, p_recv.at[other])

    first = picks[2]
    columns = [
        dot_nn(first, p_recv[r].reshape(256, 128)).T for r in range(2)
    ]
    loads[6].wait()
    power = spectrum[...]
    scale = power / (power + 0.5)
    for s in range(4):
        rows = jnp.concatenate(
            [
                columns[r][64 * t : 64 * (t + 1), 64 * s : 64 * (s + 1)]
                for r in range(2)
                for t in range(2)
            ],
            axis=1,
        ).astype(BF16)
        wiener = dot_nt(rows, leg_p[s]) * scale
        wiener_rows[s] = wiener
        partial = dot_nn(wiener.astype(BF16), leg_p[s]) * syn_scale
        back[0, s] = partial[:, :128]
        back[1, s] = partial[:, 128:]
        send(4, back.at[other, s], back_buf.at[s], core_peer)

    arrived(4, back_buf)
    both = back[g] + back_buf[...]
    halves = [
        jnp.concatenate([both[s][:, 64 * t : 64 * (t + 1)] for s in range(4)], axis=1)
        for t in range(2)
    ]
    turned = jnp.concatenate(halves, axis=0).T.astype(BF16)
    q_send[...] = dot_nn(picks[3], turned).astype(BF16).reshape(PLANE, 8, 128)
    for i, peer in plane_peers:
        send(5, q_send.at[i], q_recv.at[here], peer)
    keep(5, q_send.at[here], q_recv.at[here])
    for s in range(4):
        for p in range(4):
            for t in range(8):
                start = (p // 2) * 1024 + (p % 2) * 32 + t * 4 + s
                wiener_out[pl.Slice(start, 16, 64), :] = wiener_rows[
                    s, 16 * p : 16 * (p + 1), 128 * t : 128 * (t + 1)
                ]
    arrived(5, q_recv)
    plane = q_recv[...].reshape(256, 128)
    for h in range(2):
        turned = dot_nn(picks[4 + h, :128], plane).T.astype(BF16)
        w_send[4 * h : 4 * h + 4] = turned.reshape(4, 32, 128)
    for zl_, zh_, peer in z_peers:
        for core in (other, g):
            send(6, w_send.at[2 * zl_ + zh_], w_recv.at[g, mine], {"grp": core, **peer})
    send(6, w_send.at[mine], w_recv.at[g, mine], core_peer)
    keep(6, w_send.at[mine], w_recv.at[g, mine])
    arrived(6, w_recv)
    for r in range(2):
        for t in range(NZL):
            modes[r, :, 128 * t : 128 * (t + 1)] = (
                w_recv[r, 2 * t].astype(F32) + w_recv[r, 2 * t + 1].astype(F32)
            ).astype(BF16)

    for r in range(2):
        re, im = modes[r, :16].astype(F32), modes[r, 16:].astype(F32)
        for q in range(BLOCKS):
            i = 2 * q + r
            c, s = phase_cos[i : i + 1], phase_sin[i : i + 1]
            rotated[16 * i : 16 * (i + 1), :ORDERS] = (re * c - im * s).astype(BF16)
            rotated[16 * i : 16 * (i + 1), ORDERS:] = (-(im * c + re * s)).astype(BF16)
    for n in range(2):
        pixels = dot_nt(rotated[...], table[256 * n : 256 * (n + 1)]) * ORDERS**-0.5
        for i in range(2 * BLOCKS):
            for t in range(2):
                start = ((i // 2) * 4 + 2 * n + t) * 2 + i % 2
                signal_out[pl.Slice(start, 16, 64), :] = pixels[
                    16 * i : 16 * (i + 1), 128 * t : 128 * (t + 1)
                ]

    left(1, z_recv.at[0])
    left(1, z_recv.at[0, 0:7])
    left(2, p_recv.at[0, 0:31])
    left(3, p_recv.at[0])
    left(4, back_buf)
    left(5, q_recv.at[0:31])
    left(6, w_recv.at[0])
    left(6, w_recv.at[0, 0:7])


def store_kernel(wiener, signal, wiener_out, signal_out, sem):
    copies = []
    for i, rows in enumerate([pl.ds(512 * n, 512) for n in range(4)]):
        copies.append(pltpu.make_async_copy(wiener.at[rows], wiener_out.at[rows], sem.at[i]))
        if i < 2:
            copies.append(
                pltpu.make_async_copy(signal.at[rows], signal_out.at[rows], sem.at[4 + i])
            )
    for copy in copies:
        copy.start()
    for copy in copies:
        copy.wait()


def store(wiener, signal):
    hbm = pl.BlockSpec(memory_space=pltpu.HBM)
    block = pl.BlockSpec(memory_space=pltpu.VMEM)
    return pl.pallas_call(
        store_kernel,
        out_shape=(
            jax.ShapeDtypeStruct((2048, 128), F32),
            jax.ShapeDtypeStruct((1024, 128), F32),
        ),
        in_specs=[block] * 2,
        out_specs=(hbm, hbm),
        scratch_shapes=[pltpu.SemaphoreType.DMA((6,))],
        compiler_params=pltpu.CompilerParams(vmem_limit_bytes=16 * 1024 * 1024),
    )(wiener, signal)


def step(inputs, syn_scale):
    def vmem(shape, dtype=BF16):
        return pltpu.VMEM(shape, dtype)

    block = pl.BlockSpec(memory_space=pltpu.VMEM)
    return pl.pallas_call(
        lambda *refs: step_kernel(syn_scale, *refs),
        out_shape=(
            jax.ShapeDtypeStruct((2048, 128), F32),
            jax.ShapeDtypeStruct((1024, 128), F32),
        ),
        in_specs=[pl.BlockSpec(memory_space=pltpu.HBM)] * 8,
        out_specs=(block, block),
        scratch_shapes=[
            vmem((1024, 128), F32),
            vmem((1024, 128), F32),
            vmem((64, 128), F32),
            vmem((64, 128), jnp.int32),
            vmem((1, 2), jnp.int32),
            vmem((1, ORDERS), jnp.int32),
            vmem((1, 1024), F32),
            vmem((32 * BLOCKS, SPAN)),
            vmem((SPAN, 2 * ORDERS)),
            vmem((16, ORDERS), F32),
            vmem((16, ORDERS), F32),
            vmem((2, 2, 16, ORDERS), F32),
            vmem((4, 1024, 256)),
            vmem((4, 1024, 256)),
            vmem((2, NZL, 32, 128)),
            vmem((2, NZ, 32, 128)),
            vmem((PLANE, 8, 128)),
            vmem((2, PLANE, 8, 128)),
            vmem((2, 4, 64, 128), F32),
            vmem((4, 64, 128), F32),
            vmem((PLANE, 8, 128)),
            vmem((PLANE, 8, 128)),
            vmem((NZ, 32, 128)),
            vmem((2, NZ, 32, 128)),
            vmem((2, 32, ORDERS)),
            vmem((32 * BLOCKS, 2 * ORDERS)),
            vmem((4, 64, 1024), F32),
            vmem((6, 256, 256)),
            pltpu.SemaphoreType.DMA((7,)),
            pltpu.SemaphoreType.DMA((7,)),
            pltpu.SemaphoreType.DMA((8,)),
        ],
        compiler_params=pltpu.CompilerParams(
            collective_id=0, has_side_effects=True, vmem_limit_bytes=40000000
        ),
    )(*[pltpu.with_memory_space_constraint(a, pltpu.HBM) for a in inputs])


def per_device(
    sky_data, signal_prev, noise_var, mask_flags, cycle_table, m_table, spectrum, legendre
):
    half_len = sky_data.shape[2]
    total_l = legendre.shape[1] * lax.axis_size("grp") * lax.axis_size("real")
    syn_scale = (legendre.shape[2] / total_l) ** 0.5

    def rows(a):
        return a.reshape(-1, 2, half_len // 128, 128).swapaxes(1, 2).reshape(-1, 128)

    inputs = (
        rows(sky_data),
        rows(signal_prev),
        rows(noise_var),
        rows(mask_flags),
        cycle_table[None],
        m_table[None],
        spectrum[None],
        legendre,
    )
    wiener, signal = store(*step(inputs, syn_scale))
    wiener_alm = (
        wiener.reshape(32, 2, 8, 4, 128).transpose(0, 1, 3, 2, 4).reshape(32, 2, 4, 1024)
    )
    signal_next = signal.reshape(16, 32, 2, 128).transpose(0, 2, 1, 3).reshape(16, 2, half_len)
    return (wiener_alm, signal_next)


def solution(mesh):
    in_specs = (
        P("real", "blk", "grp"),
        P("real", "blk", "grp"),
        P("blk", "grp"),
        P("blk", "grp"),
        P("blk"),
        P(),
        P(("grp", "real")),
        P("blk", ("grp", "real"), None),
    )
    out_specs = (P(None, None, "blk", ("grp", "real")), P("real", "blk", "grp"))
    return jax.shard_map(
        per_device, mesh=mesh, in_specs=in_specs, out_specs=out_specs, check_vma=False
    )
```
